256 devices in a mesh: tm: 32 (over y, z), cell: 8 (over x, core).
Axes of the slice: x: 4, y: 4, z: 8, core: 2. Of those that a mesh axis runs over, the one named last changes fastest.
Arguments:
- increments: int32 [768, 32768], P('cell', 'tm'), may hold values from 0 to 3
- noise: bfloat16 [768, 32768], P('cell', 'tm'), may hold values from -6 to 6
- noise_scale: float32 [768], P('cell'), may hold values from 0.5 to 4
- factor: bfloat16 [32768], replicated, may hold values from 0 to 2
Outputs:
- counts: int32 [768, 32768], P('cell', 'tm')
- correlated_noise: float32 [768, 32768], P('cell', 'tm')
- total_counts: int32 [32768], P('tm')
The draws below stay inside these ranges and needn't reach their ends.
All inputs are finite; a program needn't handle non-finite values.
Results may differ from the reference program's by a relative error of at most 0.0009.
Values may be sent and summed in bfloat16 or wider, within the bound.
No kernel may reach another device: no remote copies, remote signals or barrier semaphores. Data moves between devices by JAX's collectives and lax.ppermute only.
A program may use at most 64 MiB of HBM per device.

```python
import math
import jax
import jax.numpy as jnp
from jax import lax

CELLS = 768
BLK = 512
TIME = 32768


def draw_factor(key, part):
    offsets = jnp.arange(TIME, dtype=jnp.float32)
    clamped = jnp.maximum(offsets, 1.0)
    inverse = 1.0 / clamped
    series = 1.0 - inverse / 8.0 + inverse ** 2 / 128.0 + 5.0 * inverse ** 3 / 1024.0 - 21.0 * inverse ** 4 / 32768.0
    far_value = series / jnp.sqrt(jnp.pi * clamped)
    step_range = jnp.arange(1, 32, dtype=jnp.float32)
    near_table = jnp.concatenate([jnp.ones((1,), jnp.float32), jnp.cumprod(1.0 - 0.5 / step_range)])
    near_value = near_table[jnp.minimum(jnp.arange(TIME, dtype=jnp.int32), 31)]
    baseline = jnp.where(offsets < 32.0, near_value, far_value)
    spread_key = jax.random.fold_in(key, 7)
    spread = jnp.exp(jax.random.uniform(spread_key, (TIME,), jnp.float32, math.log(0.5), math.log(2.0)))
    return (baseline * spread).astype(jnp.bfloat16)


def place_ends(result, own_key, low, largest):
    index_at = [jax.random.randint(jax.random.fold_in(own_key, axis), (), 0, length) for axis, length in enumerate(result.shape)]
    main_axis = result.shape.index(max(result.shape))
    neighbour = index_at[:main_axis] + [(index_at[main_axis] + 1) % result.shape[main_axis]] + index_at[main_axis + 1:]
    return result.at[tuple(index_at)].set(low).at[tuple(neighbour)].set(largest)


def block_scale(rng, shape, split, smallest, top_value):
    loudness = 1.0
    for axis_at, shards_of in split:
        draws = jax.random.uniform(jax.random.fold_in(jax.random.fold_in(rng, 6), axis_at), (shards_of,), jnp.float32, smallest / len(split), top_value / len(split))
        loudness = loudness * jnp.repeat(jnp.exp(draws), shape[axis_at] // shards_of).reshape((-1,) + (1,) * (len(shape) - 1 - axis_at))
    return loudness


def centred(key, extent, scale, bound, cuts=(), held_as=jnp.bfloat16):
    values = scale * jax.random.normal(key, extent, jnp.float32)
    if cuts:
        values = values * block_scale(key, extent, cuts, -0.22, 0.18)
    return jnp.clip(values, -bound, bound).astype(held_as)


def setup_inputs(seed: int = 0) -> dict:
    seeds = jax.random.split(jax.random.key(seed), 5)
    return {
        "increments": place_ends(jax.random.randint(seeds[0], (CELLS, TIME), 0, 4), jax.random.fold_in(seeds[0], 1), 0, 3).astype(jnp.int32),
        "noise": centred(seeds[1], (CELLS, TIME), 1.0, 6.0, ((0, 8), (1, 32))),
        "noise_scale": jnp.clip(jnp.exp(math.log(4.0) - 2.0794415 * jax.random.uniform(seeds[2], (CELLS,), jnp.float32) ** block_scale(seeds[2], (CELLS,), ((0, 8),), -0.2, 0.2)), 0.5, 4.0),
        "factor": draw_factor(jax.random.fold_in(seeds[4], 71), 0),
    }


def reference(increments, noise, noise_scale, factor):
    counts = jnp.cumsum(increments, axis=1, dtype=jnp.int32)
    total_counts = jnp.sum(counts, axis=0, dtype=jnp.int32)
    padded = jnp.concatenate([jnp.zeros((TIME,), jnp.float32), factor.astype(jnp.float32)])
    source = noise.astype(jnp.float32)
    pieces = []
    for target in range(TIME // BLK):
        last_col = (target + 1) * BLK
        source_ids = jnp.arange(last_col, dtype=jnp.int32)[:, None]
        target_ids = (target * BLK + jnp.arange(BLK, dtype=jnp.int32))[None, :]
        matrix = padded[(target_ids - source_ids + TIME).astype(jnp.int32)]
        pieces.append(jnp.dot(source[:, :last_col], matrix, precision=lax.Precision.HIGHEST, preferred_element_type=jnp.float32))
    convolved = jnp.concatenate(pieces, axis=1)
    correlated_noise = noise_scale[:, None] * convolved
    return counts, correlated_noise, total_counts
```

```python
import jax
import jax.numpy as jnp
from jax import lax
from jax.experimental import pallas as pl
from jax.experimental.pallas import tpu as pltpu
from jax.sharding import PartitionSpec as P

SPANS = 32
CELLS = 96
STEPS = 1024
BLK = 256
ROWS = 16
TILES = 256

VMEM = pl.BlockSpec(memory_space=pltpu.VMEM)
ANY = pl.BlockSpec(memory_space=pl.ANY)


def pack_kernel(noise_ref, inc_ref, out_ref, scr):
    x = noise_ref[...].astype(jnp.float32)
    for c in range(3):
        for g in range(4):
            for k in range(4):
                for h in range(2):
                    col = 256 * k + 128 * h
                    tile = x[32 * c + 8 * g:32 * c + 8 * g + 8, col:col + 128]
                    scr[h, pl.ds(8 * g * ROWS + 3 * k + c, 8, stride=ROWS), :] = tile
    inc = inc_ref[...].astype(jnp.float32).astype(jnp.bfloat16)
    inc = jnp.concatenate([inc, jnp.zeros((32, STEPS), jnp.bfloat16)], axis=0)
    ones = jnp.ones((8, STEPS), jnp.bfloat16)
    sums = lax.dot_general(ones, inc, (((1,), (1,)), ((), ())), preferred_element_type=jnp.float32)
    high = jnp.floor(sums * (1.0 / 64.0))
    low = sums - 64.0 * high
    zero = jnp.zeros((8, 128), jnp.float32)
    for g in range(4):
        for r, v in ((12, high), (13, low), (14, zero), (15, zero)):
            scr[0, pl.ds(8 * g * ROWS + r, 8, stride=ROWS), :] = v
            scr[1, pl.ds(8 * g * ROWS + r, 8, stride=ROWS), :] = zero
    for h in range(2):
        out_ref[:, :, 128 * h:128 * h + 128] = scr[h].astype(jnp.bfloat16).reshape(SPANS, ROWS, 128)


def table_kernel(factor_ref, tab_ref):
    row = lax.broadcasted_iota(jnp.int32, (128, 128), 0)
    col = lax.broadcasted_iota(jnp.int32, (128, 128), 1)
    keep = col >= row
    tab_ref[0] = jnp.zeros((128, 128), jnp.bfloat16)

    def rolled(l):
        line = jnp.broadcast_to(factor_ref[pl.ds(l, 1), :], (128, 128))
        return pltpu.roll(line, 0, 1, stride=1, stride_axis=0)

    def step(l, before):
        now = rolled(l)
        tab_ref[l + 1] = jnp.where(keep, now, before).astype(jnp.bfloat16)
        return now

    lax.fori_loop(0, TILES, step, jnp.zeros((128, 128), jnp.float32), unroll=4)


def local_kernel(inc_ref, counts_ref, line_ref):
    inc = inc_ref[...].astype(jnp.float32).astype(jnp.bfloat16)
    row = lax.broadcasted_iota(jnp.int32, (BLK, BLK), 0)
    col = lax.broadcasted_iota(jnp.int32, (BLK, BLK), 1)
    tri = jnp.where(row <= col, 1.0, 0.0).astype(jnp.bfloat16)
    full = jnp.ones((BLK, BLK), jnp.bfloat16)
    for k in range(4):
        mat = jnp.concatenate([full] * k + [tri], axis=0)
        part = jnp.dot(inc[:, :BLK * (k + 1)], mat, preferred_element_type=jnp.float32)
        counts_ref[:, BLK * k:BLK * (k + 1)] = part.astype(jnp.int32)
        total = jnp.sum(part, axis=0, keepdims=True)
        for h in range(2):
            line_ref[2 * k + h:2 * k + h + 1, :] = total[:, 128 * h:128 * h + 128]


def conv_kernel(recv_ref, tab_hbm, mask_ref, line_ref, out_ref, carry_ref, group_ref, tab, xf, xs, acc, sems):
    def fetch(part):
        first = 64 * part + (part > 0)
        size = 64 + (part == 0)
        return pltpu.make_async_copy(tab_hbm.at[pl.ds(first, size)], tab.at[pl.ds(first, size)], sems.at[part])

    for part in range(4):
        fetch(part).start()

    flat = recv_ref[...].reshape(SPANS * ROWS, BLK)
    xs[:, 0:BLK] = flat
    within = lax.broadcasted_iota(jnp.int32, (512, 128), 0) % ROWS
    for h in range(2):
        xf[h, 0:16, :] = jnp.zeros((16, 128), jnp.float32)
        xf[h, 16:528, :] = flat[:, 128 * h:128 * h + 128].astype(jnp.float32)
        for e in range(1, 4):
            same = xf[h, 16 - 3 * e:528 - 3 * e, :]
            prev = xf[h, 12 - 3 * e:524 - 3 * e, :]
            lane = BLK * e + 128 * h
            xs[:, lane:lane + 128] = jnp.where(within >= 3 * e, same, prev).astype(jnp.bfloat16)

    high = xf[0, pl.ds(28, SPANS, stride=ROWS), :].astype(jnp.bfloat16)
    low = xf[0, pl.ds(29, SPANS, stride=ROWS), :].astype(jnp.bfloat16)
    mask = mask_ref[...]
    dims = (((0,), (0,)), ((), ()))
    carried = 64.0 * lax.dot_general(high, mask, dims, preferred_element_type=jnp.float32)
    carried = (carried + lax.dot_general(low, mask, dims, preferred_element_type=jnp.float32))[:CELLS]
    carry_ref[...] = carried.astype(jnp.int32)
    group = (line_ref[...] + jnp.sum(carried, axis=0, keepdims=True)).astype(jnp.int32)
    for d in range(8):
        group_ref[d] = group

    acc[...] = jnp.zeros_like(acc)
    for grp in range(4):
        fetch(grp).wait()
        rows = 512 - 128 * grp

        def step(i, nothing, grp=grp, rows=rows):
            delta = 8 * grp + i
            parts = []
            for e in range(4):
                at = 2 * (4 * delta + e)
                t0, t1, t2 = tab[at], tab[at + 1], tab[at + 2]
                parts.append(jnp.concatenate([t1, t2], axis=1))
                parts.append(jnp.concatenate([t0, t1], axis=1))
            weights = jnp.concatenate(parts, axis=0)
            to = pl.ds(pl.multiple_of(ROWS * delta, ROWS), rows)
            acc[to, :] += jnp.dot(xs[0:rows, :], weights, preferred_element_type=jnp.float32)
            return nothing

        lax.fori_loop(0, 8, step, 0)

    for q in range(SPANS):
        base = ROWS * q
        for h in range(2):
            out_ref[q, 8 * h:8 * h + 8, :] = acc[base:base + 8, 128 * h:128 * h + 128]
            out_ref[q, 16 + 4 * h:20 + 4 * h, :] = acc[base + 8:base + 12, 128 * h:128 * h + 128]


def counts_kernel(counts_ref, carry_ref, groups_ref, out_ref, total_ref):
    carry = carry_ref[...]
    for j in range(8):
        out_ref[:, 128 * j:128 * j + 128] = counts_ref[:, 128 * j:128 * j + 128] + carry
    total_ref[...] = jnp.sum(groups_ref[...], axis=0)


def spread_kernel(back_ref, scale_ref, out_ref):
    for c in range(3):
        for g in range(4):
            top = 32 * c + 8 * g
            scale = jnp.broadcast_to(scale_ref[top:top + 8, :], (8, 128))
            for k in range(4):
                r = 3 * k + c
                for h in range(2):
                    sub = 8 * h + r if r < 8 else 8 + 4 * h + r
                    tile = back_ref[pl.ds(192 * g + sub, 8, stride=24), :]
                    out_ref[top:top + 8, 256 * k + 128 * h:256 * k + 128 * h + 128] = tile * scale


def call(kernel, outs, args, in_specs=None, scratch=(), name=None, flops=0):
    return pl.pallas_call(
        kernel,
        out_shape=outs,
        in_specs=in_specs or [VMEM] * len(args),
        out_specs=jax.tree.map(lambda _: VMEM, outs),
        scratch_shapes=scratch,
        name=name,
        cost_estimate=pl.CostEstimate(flops=flops, transcendentals=0, bytes_accessed=1 << 20),
    )(*args)


def shards(increments, noise, noise_scale, factor):
    f32, i32, bf16 = jnp.float32, jnp.int32, jnp.bfloat16
    sds = jax.ShapeDtypeStruct
    position = lax.axis_index("tm")
    message = call(pack_kernel, sds((SPANS, ROWS, BLK), bf16), (noise, increments),
                   scratch=[pltpu.VMEM((2, SPANS * ROWS, 128), f32)], name="pack")
    received = lax.all_to_all(message, "tm", 0, 0, tiled=True)
    table = call(table_kernel, sds((TILES + 1, 128, 128), bf16), (factor.reshape(TILES, 128).astype(f32),), name="table")
    local, line = call(local_kernel, (sds((CELLS, STEPS), i32), sds((8, 128), f32)), (increments,), name="local")
    mask = jnp.broadcast_to((jnp.arange(SPANS) < position)[:, None], (SPANS, 128)).astype(bf16)
    sent, carry, group = call(
        conv_kernel,
        (sds((SPANS, 24, 128), f32), sds((CELLS, 128), i32), sds((8, 8, 128), i32)),
        (received, table, mask, line),
        in_specs=[VMEM, ANY, VMEM, VMEM],
        scratch=[
            pltpu.VMEM((TILES + 1, 128, 128), bf16),
            pltpu.VMEM((2, 528, 128), f32),
            pltpu.VMEM((512, 4 * BLK), bf16),
            pltpu.VMEM((640, BLK), f32),
            pltpu.SemaphoreType.DMA((4,)),
        ],
        name="conv",
    )
    back = lax.all_to_all(sent, "tm", 0, 0, tiled=True)
    groups = lax.all_to_all(group, "cell", 0, 0, tiled=True)
    counts, total = call(counts_kernel, (sds((CELLS, STEPS), i32), sds((8, 128), i32)), (local, carry, groups), name="counts")
    correlated = call(spread_kernel, sds((CELLS, STEPS), f32), (back.reshape(SPANS * 24, 128), noise_scale[:, None]), name="spread")
    return counts, correlated, total.reshape(STEPS)


def solution(mesh):
    return jax.shard_map(
        shards,
        mesh=mesh,
        in_specs=(P("cell", "tm"), P("cell", "tm"), P("cell"), P()),
        out_specs=(P("cell", "tm"), P("cell", "tm"), P("tm")),
        check_vma=False,
    )
```

```python
import jax
import jax.numpy as jnp
from jax import lax
from jax.experimental import pallas as pl
from jax.experimental.pallas import tpu as pltpu
from jax.sharding import PartitionSpec as P

SPANS = 32
CELLS = 96
STEPS = 1024
BLK = 256
ROWS = 16
TILES = 256
FINE = 16
SHIFT = 3 * FINE
FAR = 128 // FINE
PART = TILES // FAR
SOON = 3

ON_CHIP = pl.BlockSpec(memory_space=pltpu.VMEM)
HBM = pl.BlockSpec(memory_space=pltpu.HBM)


def pack_kernel(noise_hbm, inc_hbm, out_hbm, x_ref, inc_ref, scr, out, sems):
    get_noise = pltpu.make_async_copy(noise_hbm, x_ref, sems.at[0])
    get_inc = pltpu.make_async_copy(inc_hbm, inc_ref, sems.at[1])
    get_inc.start()
    get_noise.start()
    get_inc.wait()
    inc = inc_ref[...].astype(jnp.float32).astype(jnp.bfloat16)
    inc = jnp.concatenate([inc, jnp.zeros((32, STEPS), jnp.bfloat16)], axis=0)
    ones = jnp.ones((8, STEPS), jnp.bfloat16)
    sums = lax.dot_general(ones, inc, (((1,), (1,)), ((), ())), preferred_element_type=jnp.float32)
    high = jnp.floor(sums * (1.0 / 64.0))
    low = sums - 64.0 * high
    zero = jnp.zeros((8, 128), jnp.float32)
    get_noise.wait()
    puts = []
    for g in range(4):
        base = 8 * g * ROWS
        for h in range(2):
            for c in range(3):
                top = 32 * c + 8 * g
                for k in range(4):
                    col = 256 * k + 128 * h
                    tile = x_ref[top:top + 8, col:col + 128].astype(jnp.float32)
                    scr[h, pl.ds(base + 3 * k + c, 8, stride=ROWS), :] = tile
            for r, v in ((12, high), (13, low), (14, zero), (15, zero)):
                scr[h, pl.ds(base + r, 8, stride=ROWS), :] = v if h == 0 else zero
            tile = scr[h, base:base + 8 * ROWS, :].astype(jnp.bfloat16)
            out[8 * g:8 * g + 8, :, 128 * h:128 * h + 128] = tile.reshape(8, ROWS, 128)
        some = pl.ds(8 * g, 8)
        puts.append(pltpu.make_async_copy(out.at[some], out_hbm.at[some], sems.at[2 + g]))
        puts[-1].start()
    for put in puts:
        put.wait()


def table_kernel(factor_ref, inc_hbm, tab_ref, counts_ref, line_ref, lines, inc_ref, sem):
    step = pl.program_id(0)
    first = step * PART
    get_inc = pltpu.make_async_copy(inc_hbm, inc_ref, sem.at[0])

    @pl.when(step == 0)
    def _():
        get_inc.start()
        lines[0:8, :] = jnp.zeros((8, 128), jnp.float32)
        lines[8:8 + TILES, :] = factor_ref[...].astype(jnp.float32)

    row = lax.broadcasted_iota(jnp.int32, (128, 128), 0)
    col = lax.broadcasted_iota(jnp.int32, (128, 128), 1)
    keep = col >= row

    def rolled(at):
        line = jnp.broadcast_to(lines[pl.ds(at, 1), :], (128, 128))
        return pltpu.roll(line, 0, 1, stride=1, stride_axis=0)

    before = rolled(first + 7)
    for i in range(PART):
        now = rolled(first + 8 + i)
        tab_ref[i] = jnp.where(keep, now, before).astype(jnp.bfloat16)
        before = now

    @pl.when(step == FAR - 1)
    def _():
        get_inc.wait()
        inc = inc_ref[...].astype(jnp.float32).astype(jnp.bfloat16)
        row = lax.broadcasted_iota(jnp.int32, (BLK, BLK), 0)
        col = lax.broadcasted_iota(jnp.int32, (BLK, BLK), 1)
        tri = jnp.where(row <= col, 1.0, 0.0).astype(jnp.bfloat16)
        full = jnp.ones((BLK, BLK), jnp.bfloat16)
        for k in range(4):
            mat = jnp.concatenate([full] * k + [tri], axis=0)
            part = jnp.dot(inc[:, :BLK * (k + 1)], mat, preferred_element_type=jnp.float32)
            counts_ref[:, BLK * k:BLK * (k + 1)] = part.astype(jnp.int32)
            total = jnp.sum(part, axis=0, keepdims=True)
            for h in range(2):
                line_ref[2 * k + h:2 * k + h + 1, :] = total[:, 128 * h:128 * h + 128]


def conv_kernel(recv_ref, tab_hbm, out_ref, tab, xf, xs, acc, sems):
    def fetch(part):
        lanes = pl.ds(PART * part, PART)
        return pltpu.make_async_copy(tab_hbm.at[lanes], tab.at[lanes], sems.at[part])

    for part in range(FAR):
        fetch(part).start()

    xf[:, 0:SHIFT, :] = jnp.zeros((2, SHIFT, 128), jnp.float32)
    for h in range(2):
        lanes = slice(128 * h, 128 * h + 128)
        for q in range(SPANS):
            xf[h, SHIFT + 12 * q:SHIFT + 12 * q + 12, :] = recv_ref[q, 0:12, lanes].astype(jnp.float32)
    for e in range(FINE):
        for h in range(2):
            lane = BLK * e + 128 * h
            xs[:, lane:lane + 128] = xf[h, SHIFT - 3 * e:SHIFT - 3 * e + 384, :].astype(jnp.bfloat16)

    for far in range(FAR):
        if far in (0, SOON):
            for part in range(far, SOON if far == 0 else FAR):
                fetch(part).wait()
        rows = 384 - SHIFT * far
        parts = []
        for e in range(FINE):
            at = 2 * (FINE * far + e)
            t0 = tab[at - 1] if at else jnp.zeros((128, 128), jnp.bfloat16)
            t1, t2 = tab[at], tab[at + 1]
            parts.append(jnp.concatenate([t1, t2], axis=1))
            parts.append(jnp.concatenate([t0, t1], axis=1))
        weights = jnp.concatenate(parts, axis=0)
        part = jnp.dot(xs[0:rows, :], weights, preferred_element_type=jnp.float32)
        if far == 0:
            acc[...] = part
        else:
            acc[SHIFT * far:, :] += part
        for q in range(4 * far, 4 * far + 4):
            for h in range(2):
                for r in range(0, 12, 4):
                    to = 8 * h + r if r < 8 else 16 + 4 * h
                    out_ref[q, to:to + 4, :] = acc[12 * q + r:12 * q + r + 4, 128 * h:128 * h + 128]


def carry_kernel(recv_ref, line_ref, carry_ref, group_ref):
    sums = recv_ref[:, 12:14, 0:128].astype(jnp.float32)
    high = sums[:, 0, :].astype(jnp.bfloat16)
    low = sums[:, 1, :].astype(jnp.bfloat16)
    span = lax.broadcasted_iota(jnp.int32, (SPANS, 128), 0)
    mask = jnp.where(span < lax.axis_index("tm"), 1.0, 0.0).astype(jnp.bfloat16)
    dims = (((0,), (0,)), ((), ()))
    carried = 64.0 * lax.dot_general(high, mask, dims, preferred_element_type=jnp.float32)
    carried = (carried + lax.dot_general(low, mask, dims, preferred_element_type=jnp.float32))[:CELLS]
    carry_ref[...] = carried.astype(jnp.int32)
    group_ref[...] = (line_ref[...] + jnp.sum(carried, axis=0, keepdims=True)).astype(jnp.int32)


def counts_kernel(counts_ref, carry_ref, a_ref, b_ref, c_ref, d_ref, out_ref, total_ref):
    carry = carry_ref[...]
    for j in range(8):
        out_ref[:, 128 * j:128 * j + 128] = counts_ref[:, 128 * j:128 * j + 128] + carry
    total_ref[...] = (a_ref[...] + b_ref[...]) + (c_ref[...] + d_ref[...])


def spread_kernel(back_ref, scale_ref, out_hbm, out, sems):
    copies = []
    for g in range(4):
        for c in range(3):
            top = 32 * c + 8 * g
            scale = jnp.broadcast_to(scale_ref[top:top + 8, :], (8, 128))
            for k in range(4):
                r = 3 * k + c
                for h in range(2):
                    sub = 8 * h + r if r < 8 else 8 + 4 * h + r
                    tile = back_ref[pl.ds(192 * g + sub, 8, stride=24), :]
                    out[top:top + 8, 256 * k + 128 * h:256 * k + 128 * h + 128] = tile * scale
            rows = pl.ds(top, 8)
            copies.append(pltpu.make_async_copy(out.at[rows], out_hbm.at[rows], sems.at[len(copies)]))
            copies[-1].start()
    for copy in copies:
        copy.wait()


def call(kernel, outs, args, in_specs=None, out_specs=None, scratch=(), **rest):
    return pl.pallas_call(
        kernel,
        out_shape=outs,
        in_specs=in_specs or [ON_CHIP] * len(args),
        out_specs=out_specs or jax.tree.map(lambda _: ON_CHIP, outs),
        scratch_shapes=scratch,
        compiler_params=pltpu.CompilerParams(vmem_limit_bytes=24 << 20),
        **rest,
    )(*args)


def on_chip(x):
    return pltpu.with_memory_space_constraint(x, pltpu.VMEM)


def in_hbm(x):
    return pltpu.with_memory_space_constraint(x, pltpu.HBM)


def steps(increments, noise, noise_scale, factor):
    f32, i32, bf16 = jnp.float32, jnp.int32, jnp.bfloat16
    sds = jax.ShapeDtypeStruct
    dma = pltpu.SemaphoreType.DMA
    message = call(
        pack_kernel, sds((SPANS, ROWS, BLK), bf16), (in_hbm(noise), in_hbm(increments)),
        in_specs=[HBM, HBM], out_specs=HBM,
        scratch=[pltpu.VMEM((CELLS, STEPS), bf16), pltpu.VMEM((CELLS, STEPS), i32),
                 pltpu.VMEM((2, SPANS * ROWS, 128), f32), pltpu.VMEM((SPANS, ROWS, BLK), bf16), dma((6,))],
    )
    received = lax.all_to_all(message, "tm", 0, 0, tiled=True)
    whole = lambda i: (0, 0)
    table, local, line = call(
        table_kernel,
        (pltpu.HBM((TILES, 128, 128), bf16), sds((CELLS, STEPS), i32), sds((8, 128), f32)),
        (in_hbm(factor.reshape(TILES, 128)), in_hbm(increments)),
        grid=(FAR,),
        in_specs=[pl.BlockSpec((TILES, 128), whole), HBM],
        out_specs=(pl.BlockSpec((PART, 128, 128), lambda i: (i, 0, 0)),
                   pl.BlockSpec((CELLS, STEPS), whole), pl.BlockSpec((8, 128), whole)),
        scratch=[pltpu.VMEM((8 + TILES, 128), f32), pltpu.VMEM((CELLS, STEPS), i32), dma((1,))],
    )
    sent = call(
        conv_kernel, sds((SPANS, 24, 128), f32), (on_chip(received), in_hbm(table)),
        in_specs=[ON_CHIP, HBM],
        scratch=[
            pltpu.VMEM((TILES, 128, 128), bf16),
            pltpu.VMEM((2, SHIFT + 384, 128), f32),
            pltpu.VMEM((384, FINE * BLK), bf16),
            pltpu.VMEM((384, BLK), f32),
            dma((FAR,)),
        ],
    )
    back = lax.all_to_all(sent, "tm", 0, 0, tiled=True)
    carry, group = call(carry_kernel, (sds((CELLS, 128), i32), sds((8, 128), i32)), (received, line))
    group = group + lax.ppermute(group, "cell", [(i, i ^ 1) for i in range(8)])
    others = [lax.ppermute(group, "cell", [(i, (i + 2 * k) % 8) for i in range(8)]) for k in (1, 2, 3)]
    counts, total = call(
        counts_kernel, (sds((CELLS, STEPS), i32), sds((8, 128), i32)), (local, carry, group, *others))
    correlated = call(
        spread_kernel, sds((CELLS, STEPS), f32), (on_chip(back.reshape(SPANS * 24, 128)), noise_scale[:, None]),
        out_specs=HBM, scratch=[pltpu.VMEM((CELLS, STEPS), f32), dma((12,))],
    )
    return counts, correlated, total.reshape(STEPS)


def solution(mesh):
    return jax.shard_map(
        steps,
        mesh=mesh,
        in_specs=(P("cell", "tm"), P("cell", "tm"), P("cell"), P()),
        out_specs=(P("cell", "tm"), P("cell", "tm"), P("tm")),
        check_vma=False,
    )
```

```python
import jax
import jax.numpy as jnp
from jax import lax
from jax.experimental import pallas as pl
from jax.experimental.pallas import tpu as pltpu
from jax.sharding import PartitionSpec as P

SPANS = 32
CELLS = 96
STEPS = 1024
BLK = 256
ROWS = 16
TILES = 256
FINE = 16
SHIFT = 3 * FINE
STRIDE = 5
ORDER = [STRIDE * p % SPANS for p in range(SPANS)]
PLACE = [ORDER.index(q) for q in range(SPANS)]
FAR = 128 // FINE

ON_CHIP = pl.BlockSpec(memory_space=pltpu.VMEM)
HBM = pl.BlockSpec(memory_space=pltpu.HBM)


def pack_kernel(noise_hbm, inc_hbm, factor_hbm, out, strip_ref, x_ref, inc_ref, factor_ref, lines, scr, sems):
    get_noise = pltpu.make_async_copy(noise_hbm, x_ref, sems.at[0])
    get_inc = pltpu.make_async_copy(inc_hbm, inc_ref, sems.at[1])
    get_factor = pltpu.make_async_copy(factor_hbm, factor_ref, sems.at[2])
    get_factor.start()
    get_inc.start()
    get_noise.start()

    get_factor.wait()
    lines[...] = factor_ref[...].astype(jnp.float32)
    row = lax.broadcasted_iota(jnp.int32, (16, 128), 0)
    col = lax.broadcasted_iota(jnp.int32, (16, 128), 1)
    keep = col >= row
    before = jnp.zeros((16, 128), jnp.float32)
    for tile in range(TILES):
        line = jnp.broadcast_to(lines[tile:tile + 1, :], (16, 128))
        now = pltpu.roll(line, 0, 1, stride=1, stride_axis=0)
        strip_ref[tile] = jnp.where(keep, now, before).astype(jnp.bfloat16)
        before = now

    get_inc.wait()
    inc = inc_ref[...].astype(jnp.float32).astype(jnp.bfloat16)
    inc = jnp.concatenate([inc, jnp.zeros((32, STEPS), jnp.bfloat16)], axis=0)
    ones = jnp.ones((8, STEPS), jnp.bfloat16)
    sums = lax.dot_general(ones, inc, (((1,), (1,)), ((), ())), preferred_element_type=jnp.float32)
    high = jnp.floor(sums * (1.0 / 64.0))
    low = sums - 64.0 * high
    zero = jnp.zeros((8, 128), jnp.float32)
    get_noise.wait()
    for g in range(4):
        base = 8 * g * ROWS
        for h in range(2):
            for c in range(3):
                top = 32 * c + 8 * g
                for k in range(4):
                    col = 256 * k + 128 * h
                    tile = x_ref[top:top + 8, col:col + 128].astype(jnp.float32)
                    scr[h, pl.ds(base + 3 * k + c, 8, stride=ROWS), :] = tile
            for r, v in ((12, high), (13, low), (14, zero), (15, zero)):
                scr[h, pl.ds(base + r, 8, stride=ROWS), :] = v if h == 0 else zero
            tile = scr[h, base:base + 8 * ROWS, :].astype(jnp.bfloat16)
            out[8 * g:8 * g + 8, :, 128 * h:128 * h + 128] = tile.reshape(8, ROWS, 128)


def local_kernel(inc_hbm, counts_ref, line_ref, inc_ref, sem):
    get_inc = pltpu.make_async_copy(inc_hbm, inc_ref, sem.at[0])
    get_inc.start()
    row = lax.broadcasted_iota(jnp.int32, (BLK, BLK), 0)
    col = lax.broadcasted_iota(jnp.int32, (BLK, BLK), 1)
    tri = jnp.where(row <= col, 1.0, 0.0).astype(jnp.bfloat16)
    full = jnp.ones((BLK, BLK), jnp.bfloat16)
    get_inc.wait()
    inc = inc_ref[...].astype(jnp.float32).astype(jnp.bfloat16)
    for k in range(4):
        mat = jnp.concatenate([full] * k + [tri], axis=0)
        part = jnp.dot(inc[:, :BLK * (k + 1)], mat, preferred_element_type=jnp.float32)
        counts_ref[:, BLK * k:BLK * (k + 1)] = part.astype(jnp.int32)
        total = jnp.sum(part, axis=0, keepdims=True)
        for h in range(2):
            line_ref[2 * k + h:2 * k + h + 1, :] = total[:, 128 * h:128 * h + 128]


def conv_kernel(recv_ref, strip, out_ref, xf, xs, acc):
    xf[:, 0:SHIFT, :] = jnp.zeros((2, SHIFT, 128), jnp.float32)
    for h in range(2):
        lanes = slice(128 * h, 128 * h + 128)
        for q in range(SPANS):
            xf[h, SHIFT + 12 * q:SHIFT + 12 * q + 12, :] = recv_ref[PLACE[q], 0:12, lanes].astype(jnp.float32)
    for e in range(FINE):
        for h in range(2):
            lane = BLK * e + 128 * h
            xs[:, lane:lane + 128] = xf[h, SHIFT - 3 * e:SHIFT - 3 * e + 384, :].astype(jnp.bfloat16)

    col = lax.broadcasted_iota(jnp.int32, (16, 128), 1)
    zero = jnp.zeros((16, 128), jnp.bfloat16)

    def rolls(tile):
        if tile < 0:
            return [zero] * 8
        base = strip[tile]
        return [base] + [pltpu.roll(base, 16 * i, 1) for i in range(1, 8)]

    def square(now, before):
        return jnp.concatenate(
            [now[0]] + [jnp.where(col >= 16 * i, now[i], before[i]) for i in range(1, 8)], axis=0)

    for far in range(FAR):
        rows = 384 - SHIFT * far
        first = 2 * FINE * far
        rolled = {tile: rolls(tile) for tile in range(first - 2, first + 2 * FINE)}
        squares = {tile: square(rolled[tile], rolled[tile - 1]) for tile in range(first - 1, first + 2 * FINE)}
        parts = []
        for e in range(FINE):
            at = first + 2 * e
            parts.append(jnp.concatenate([squares[at], squares[at + 1]], axis=1))
            parts.append(jnp.concatenate([squares[at - 1], squares[at]], axis=1))
        weights = jnp.concatenate(parts, axis=0)
        part = jnp.dot(xs[0:rows, :], weights, preferred_element_type=jnp.float32)
        if far == 0:
            acc[...] = part
        else:
            acc[SHIFT * far:, :] += part
        for q in range(4 * far, 4 * far + 4):
            for h in range(2):
                for r in range(0, 12, 4):
                    to = 8 * h + r if r < 8 else 16 + 4 * h
                    out_ref[PLACE[q], to:to + 4, :] = acc[12 * q + r:12 * q + r + 4, 128 * h:128 * h + 128]


def carry_kernel(recv_ref, line_ref, carry_ref, group_ref):
    sums = recv_ref[:, 12:14, 0:128].astype(jnp.float32)
    high = sums[:, 0, :].astype(jnp.bfloat16)
    low = sums[:, 1, :].astype(jnp.bfloat16)
    span = STRIDE * lax.broadcasted_iota(jnp.int32, (SPANS, 128), 0) % SPANS
    mask = jnp.where(span < lax.axis_index("tm"), 1.0, 0.0).astype(jnp.bfloat16)
    dims = (((0,), (0,)), ((), ()))
    carried = 64.0 * lax.dot_general(high, mask, dims, preferred_element_type=jnp.float32)
    carried = (carried + lax.dot_general(low, mask, dims, preferred_element_type=jnp.float32))[:CELLS]
    carry_ref[...] = carried.astype(jnp.int32)
    group_ref[...] = (line_ref[...] + jnp.sum(carried, axis=0, keepdims=True)).astype(jnp.int32)


def counts_kernel(counts_ref, carry_ref, out_ref):
    carry = carry_ref[...]
    for j in range(8):
        out_ref[:, 128 * j:128 * j + 128] = counts_ref[:, 128 * j:128 * j + 128] + carry


def spread_kernel(back_ref, scale_ref, out_hbm, out, sems):
    copies = []
    for g in range(4):
        for c in range(3):
            top = 32 * c + 8 * g
            scale = jnp.broadcast_to(scale_ref[top:top + 8, :], (8, 128))
            for k in range(4):
                r = 3 * k + c
                for h in range(2):
                    sub = 8 * h + r if r < 8 else 8 + 4 * h + r
                    tile = back_ref[pl.ds(192 * g + sub, 8, stride=24), :]
                    out[top:top + 8, 256 * k + 128 * h:256 * k + 128 * h + 128] = tile * scale
            rows = pl.ds(top, 8)
            copies.append(pltpu.make_async_copy(out.at[rows], out_hbm.at[rows], sems.at[len(copies)]))
            copies[-1].start()
    for copy in copies:
        copy.wait()


def call(kernel, outs, args, in_specs=None, out_specs=None, scratch=(), **rest):
    return pl.pallas_call(
        kernel,
        out_shape=outs,
        in_specs=in_specs or [ON_CHIP] * len(args),
        out_specs=out_specs or jax.tree.map(lambda _: ON_CHIP, outs),
        scratch_shapes=scratch,
        compiler_params=pltpu.CompilerParams(vmem_limit_bytes=24 << 20),
        **rest,
    )(*args)


def on_chip(x):
    return pltpu.with_memory_space_constraint(x, pltpu.VMEM)


def in_hbm(x):
    return pltpu.with_memory_space_constraint(x, pltpu.HBM)


def steps(increments, noise, noise_scale, factor):
    f32, i32, bf16 = jnp.float32, jnp.int32, jnp.bfloat16
    sds = jax.ShapeDtypeStruct
    dma = pltpu.SemaphoreType.DMA
    chip = pltpu.VMEM
    message, strips = call(
        pack_kernel, (sds((SPANS, ROWS, BLK), bf16), chip((TILES, 16, 128), bf16)),
        (in_hbm(noise), in_hbm(increments), in_hbm(factor.reshape(TILES, 128))), in_specs=[HBM, HBM, HBM],
        scratch=[pltpu.VMEM((CELLS, STEPS), bf16), pltpu.VMEM((CELLS, STEPS), i32), pltpu.VMEM((TILES, 128), bf16),
                 pltpu.VMEM((TILES, 128), f32), pltpu.VMEM((2, SPANS * ROWS, 128), f32), dma((3,))],
    )
    received = lax.all_to_all(message, "tm", 0, 0, tiled=True, axis_index_groups=[ORDER])
    sent = call(
        conv_kernel, sds((SPANS, 24, 128), f32), (on_chip(received), on_chip(strips)),
        scratch=[
            pltpu.VMEM((2, SHIFT + 384, 128), f32),
            pltpu.VMEM((384, FINE * BLK), bf16),
            pltpu.VMEM((384, BLK), f32),
        ],
    )
    back = lax.all_to_all(sent, "tm", 0, 0, tiled=True, axis_index_groups=[ORDER])
    local, line = call(
        local_kernel, (sds((CELLS, STEPS), i32), sds((8, 128), f32)), (in_hbm(increments),), in_specs=[HBM],
        scratch=[pltpu.VMEM((CELLS, STEPS), i32), dma((1,))])
    carry, group = call(carry_kernel, (sds((CELLS, 128), i32), sds((8, 128), i32)), (received, line))
    group = group + lax.ppermute(group, "cell", [(i, i ^ 1) for i in range(8)])
    others = [lax.ppermute(group, "cell", [(i, (i + 2 * k) % 8) for i in range(8)]) for k in (1, 2, 3)]
    counts = call(counts_kernel, sds((CELLS, STEPS), i32), (local, carry))
    total = group + others[0] + others[1] + others[2]
    correlated = call(
        spread_kernel, sds((CELLS, STEPS), f32), (on_chip(back.reshape(SPANS * 24, 128)), noise_scale[:, None]),
        out_specs=HBM, scratch=[pltpu.VMEM((CELLS, STEPS), f32), dma((12,))],
    )
    return counts, correlated, total.reshape(STEPS)


def solution(mesh):
    return jax.shard_map(
        steps,
        mesh=mesh,
        in_specs=(P("cell", "tm"), P("cell", "tm"), P("cell"), P()),
        out_specs=(P("cell", "tm"), P("cell", "tm"), P("tm")),
        check_vma=False,
    )
```

```python
import math

import jax
import jax.numpy as jnp
from jax import lax
from jax.experimental import pallas as pl
from jax.experimental.pallas import tpu as pltpu
from jax.sharding import PartitionSpec as P

SPANS = 32
CELLS = 96
STEPS = 1024
BLK = 256
ROWS = 16
TILES = 256
FINE = 16
SHIFT = 3 * FINE
LOG_TOP = math.log2(32000.0)
TINY = 2.0 ** -100
STRIDE = 5
FIRST = 31
ORDER = [(STRIDE * p + FIRST) % SPANS for p in range(SPANS)]
PLACE = [ORDER.index(q) for q in range(SPANS)]
FAR = 128 // FINE

ON_CHIP = pl.BlockSpec(memory_space=pltpu.VMEM)
HBM = pl.BlockSpec(memory_space=pltpu.HBM)


def pack_kernel(noise_hbm, inc_hbm, factor_hbm, out, strip_ref, small_ref, x_ref, inc_ref, factor_ref, lines, scr, sems):
    get_noise = pltpu.make_async_copy(noise_hbm, x_ref, sems.at[0])
    get_inc = pltpu.make_async_copy(inc_hbm, inc_ref, sems.at[1])
    get_factor = pltpu.make_async_copy(factor_hbm, factor_ref, sems.at[2])
    get_factor.start()
    get_inc.start()
    get_noise.start()

    get_factor.wait()
    lines[...] = factor_ref[...].astype(jnp.float32)
    row = lax.broadcasted_iota(jnp.int32, (16, 128), 0)
    col = lax.broadcasted_iota(jnp.int32, (16, 128), 1)
    keep = col >= row
    before = jnp.zeros((16, 128), jnp.float32)
    for tile in range(TILES):
        line = jnp.broadcast_to(lines[tile:tile + 1, :], (16, 128))
        now = pltpu.roll(line, 0, 1, stride=1, stride_axis=0)
        strip_ref[tile] = jnp.where(keep, now, before).astype(jnp.bfloat16)
        before = now

    get_inc.wait()
    inc = inc_ref[...].astype(jnp.float32).astype(jnp.bfloat16)
    small_ref[...] = inc
    inc = jnp.concatenate([inc, jnp.zeros((32, STEPS), jnp.bfloat16)], axis=0)
    ones = jnp.ones((8, STEPS), jnp.bfloat16)
    sums = lax.dot_general(ones, inc, (((1,), (1,)), ((), ())), preferred_element_type=jnp.float32)
    high = jnp.floor(sums * (1.0 / 64.0))
    low = sums - 64.0 * high
    zero = jnp.zeros((8, 128), jnp.float32)
    get_noise.wait()
    for g in range(4):
        base = 8 * g * ROWS
        for h in range(2):
            for c in range(3):
                top = 32 * c + 8 * g
                for k in range(4):
                    col = 256 * k + 128 * h
                    tile = x_ref[top:top + 8, col:col + 128].astype(jnp.float32)
                    scr[h, pl.ds(base + 3 * k + c, 8, stride=ROWS), :] = tile
            for r, v in ((12, high), (13, low), (14, zero), (15, zero)):
                scr[h, pl.ds(base + r, 8, stride=ROWS), :] = v if h == 0 else zero
            tile = scr[h, base:base + 8 * ROWS, :].astype(jnp.bfloat16)
            out[8 * g:8 * g + 8, :, 128 * h:128 * h + 128] = tile.reshape(8, ROWS, 128)


def local_kernel(small_ref, counts_ref, line_ref):
    row = lax.broadcasted_iota(jnp.int32, (BLK, BLK), 0)
    col = lax.broadcasted_iota(jnp.int32, (BLK, BLK), 1)
    tri = jnp.where(row <= col, 1.0, 0.0).astype(jnp.bfloat16)
    full = jnp.ones((BLK, BLK), jnp.bfloat16)
    inc = small_ref[...]
    for k in range(4):
        mat = jnp.concatenate([full] * k + [tri], axis=0)
        part = jnp.dot(inc[:, :BLK * (k + 1)], mat, preferred_element_type=jnp.float32)
        counts_ref[:, BLK * k:BLK * (k + 1)] = part.astype(jnp.int32)
        total = jnp.sum(part, axis=0, keepdims=True)
        for h in range(2):
            line_ref[2 * k + h:2 * k + h + 1, :] = total[:, 128 * h:128 * h + 128]


def conv_kernel(recv_ref, strip, out_ref, xf, xs, acc):
    xf[:, 0:SHIFT, :] = jnp.zeros((2, SHIFT, 128), jnp.float32)
    for h in range(2):
        lanes = slice(128 * h, 128 * h + 128)
        for q in range(SPANS):
            xf[h, SHIFT + 12 * q:SHIFT + 12 * q + 12, :] = recv_ref[PLACE[q], 0:12, lanes].astype(jnp.float32)
    for e in range(FINE):
        for h in range(2):
            lane = BLK * e + 128 * h
            xs[:, lane:lane + 128] = xf[h, SHIFT - 3 * e:SHIFT - 3 * e + 384, :].astype(jnp.bfloat16)

    col = lax.broadcasted_iota(jnp.int32, (16, 128), 1)
    zero = jnp.zeros((16, 128), jnp.bfloat16)

    def rolls(tile):
        if tile < 0:
            return [zero] * 8
        base = strip[tile]
        return [base] + [pltpu.roll(base, 16 * i, 1) for i in range(1, 8)]

    def square(now, before):
        return jnp.concatenate(
            [now[0]] + [jnp.where(col >= 16 * i, now[i], before[i]) for i in range(1, 8)], axis=0)

    for far in range(FAR):
        rows = 384 - SHIFT * far
        first = 2 * FINE * far
        rolled = {tile: rolls(tile) for tile in range(first - 2, first + 2 * FINE)}
        squares = {tile: square(rolled[tile], rolled[tile - 1]) for tile in range(first - 1, first + 2 * FINE)}
        parts = []
        for e in range(FINE):
            at = first + 2 * e
            parts.append(jnp.concatenate([squares[at], squares[at + 1]], axis=1))
            parts.append(jnp.concatenate([squares[at - 1], squares[at]], axis=1))
        weights = jnp.concatenate(parts, axis=0)
        part = jnp.dot(xs[0:rows, :], weights, preferred_element_type=jnp.float32)
        if far == 0:
            acc[...] = part
        else:
            acc[SHIFT * far:, :] += part
        for q in range(4 * far, 4 * far + 4):
            top, low = slice(12 * q, 12 * q + 8), slice(12 * q + 8, 12 * q + 12)
            values = [acc[top, 0:128], acc[top, 128:256], jnp.concatenate([acc[low, 0:128], acc[low, 128:256]], axis=0)]
            most = jnp.maximum(jnp.maximum(jnp.abs(values[0]), jnp.abs(values[1])), jnp.abs(values[2]))
            most = jnp.maximum(jnp.max(most, axis=1, keepdims=True), TINY)
            power = jnp.broadcast_to(jnp.ceil(jnp.log2(most) - LOG_TOP), (8, 128))
            unit = jnp.exp2(-power)
            coded = [jnp.round(v * unit) for v in values] + [power]
            for half in range(2):
                rows16 = jnp.concatenate(coded[2 * half:2 * half + 2], axis=0)
                out_ref[PLACE[q], 16 * half:16 * half + 16, :] = rows16.astype(jnp.int32).astype(jnp.int16)


def carry_kernel(recv_ref, line_ref, carry_ref, group_ref):
    sums = recv_ref[:, 12:14, 0:128].astype(jnp.float32)
    high = sums[:, 0, :].astype(jnp.bfloat16)
    low = sums[:, 1, :].astype(jnp.bfloat16)
    span = (STRIDE * lax.broadcasted_iota(jnp.int32, (SPANS, 128), 0) + FIRST) % SPANS
    mask = jnp.where(span < lax.axis_index("tm"), 1.0, 0.0).astype(jnp.bfloat16)
    dims = (((0,), (0,)), ((), ()))
    carried = 64.0 * lax.dot_general(high, mask, dims, preferred_element_type=jnp.float32)
    carried = (carried + lax.dot_general(low, mask, dims, preferred_element_type=jnp.float32))[:CELLS]
    carry_ref[...] = carried.astype(jnp.int32)
    group_ref[...] = (line_ref[...] + jnp.sum(carried, axis=0, keepdims=True)).astype(jnp.int32)


def counts_kernel(counts_ref, carry_ref, out_ref):
    carry = carry_ref[...]
    for j in range(8):
        out_ref[:, 128 * j:128 * j + 128] = counts_ref[:, 128 * j:128 * j + 128] + carry


def spread_kernel(back_ref, scale_ref, out_hbm, flat, out, sems):
    copies = []
    for g in range(4):
        base = 256 * g
        flat[base:base + 256, :] = back_ref[base:base + 256, :].astype(jnp.int32).astype(jnp.float32)
        units = [jnp.exp2(flat[pl.ds(base + 24 + j, 8, stride=32), :]) for j in range(8)]
        for c in range(3):
            top = 32 * c + 8 * g
            scale = jnp.broadcast_to(scale_ref[top:top + 8, :], (8, 128))
            for k in range(4):
                r = 3 * k + c
                for h in range(2):
                    sub = 8 * h + r if r < 8 else 8 + 4 * h + r
                    tile = flat[pl.ds(base + sub, 8, stride=32), :] * units[sub % 8]
                    out[top:top + 8, 256 * k + 128 * h:256 * k + 128 * h + 128] = tile * scale
            rows = pl.ds(top, 8)
            copies.append(pltpu.make_async_copy(out.at[rows], out_hbm.at[rows], sems.at[len(copies)]))
            copies[-1].start()
    for copy in copies:
        copy.wait()


def call(kernel, outs, args, in_specs=None, out_specs=None, scratch=(), **rest):
    return pl.pallas_call(
        kernel,
        out_shape=outs,
        in_specs=in_specs or [ON_CHIP] * len(args),
        out_specs=out_specs or jax.tree.map(lambda _: ON_CHIP, outs),
        scratch_shapes=scratch,
        compiler_params=pltpu.CompilerParams(vmem_limit_bytes=24 << 20),
        **rest,
    )(*args)


def on_chip(x):
    return pltpu.with_memory_space_constraint(x, pltpu.VMEM)


def in_hbm(x):
    return pltpu.with_memory_space_constraint(x, pltpu.HBM)


def steps(increments, noise, noise_scale, factor):
    f32, i32, bf16 = jnp.float32, jnp.int32, jnp.bfloat16
    sds = jax.ShapeDtypeStruct
    dma = pltpu.SemaphoreType.DMA
    chip = pltpu.VMEM
    message, strips, small = call(
        pack_kernel, (sds((SPANS, ROWS, BLK), bf16), chip((TILES, 16, 128), bf16), chip((CELLS, STEPS), bf16)),
        (in_hbm(noise), in_hbm(increments), in_hbm(factor.reshape(TILES, 128))), in_specs=[HBM, HBM, HBM],
        scratch=[pltpu.VMEM((CELLS, STEPS), bf16), pltpu.VMEM((CELLS, STEPS), i32), pltpu.VMEM((TILES, 128), bf16),
                 pltpu.VMEM((TILES, 128), f32), pltpu.VMEM((2, SPANS * ROWS, 128), f32), dma((3,))],
    )
    received = lax.all_to_all(message, "tm", 0, 0, tiled=True, axis_index_groups=[ORDER])
    sent = call(
        conv_kernel, sds((SPANS, 32, 128), jnp.int16), (on_chip(received), on_chip(strips)),
        scratch=[
            pltpu.VMEM((2, SHIFT + 384, 128), f32),
            pltpu.VMEM((384, FINE * BLK), bf16),
            pltpu.VMEM((384, BLK), f32),
        ],
    )
    back = lax.all_to_all(sent, "tm", 0, 0, tiled=True, axis_index_groups=[ORDER])
    local, line = call(local_kernel, (sds((CELLS, STEPS), i32), sds((8, 128), f32)), (small,))
    carry, group = call(carry_kernel, (sds((CELLS, 128), i32), sds((8, 128), i32)), (received, line))
    group = group + lax.ppermute(group, "cell", [(i, i ^ 1) for i in range(8)])
    others = [lax.ppermute(group, "cell", [(i, (i + 2 * k) % 8) for i in range(8)]) for k in (1, 2, 3)]
    counts = call(counts_kernel, sds((CELLS, STEPS), i32), (local, carry))
    total = group + others[0] + others[1] + others[2]
    correlated = call(
        spread_kernel, sds((CELLS, STEPS), f32), (on_chip(back.reshape(SPANS * 32, 128)), noise_scale[:, None]),
        out_specs=HBM, scratch=[pltpu.VMEM((SPANS * 32, 128), f32), pltpu.VMEM((CELLS, STEPS), f32), dma((12,))],
    )
    return counts, correlated, total.reshape(STEPS)


def solution(mesh):
    return jax.shard_map(
        steps,
        mesh=mesh,
        in_specs=(P("cell", "tm"), P("cell", "tm"), P("cell"), P()),
        out_specs=(P("cell", "tm"), P("cell", "tm"), P("tm")),
        check_vma=False,
    )
```

```python
import math

import jax
import jax.numpy as jnp
from jax import lax
from jax.experimental import pallas as pl
from jax.experimental.pallas import tpu as pltpu
from jax.sharding import PartitionSpec as P

SPANS = 32
CELLS = 96
STEPS = 1024
BLK = 256
ROWS = 16
TILES = 256
FINE = 16
SHIFT = 3 * FINE
LOG_TOP = math.log2(32000.0)
TINY = 2.0 ** -100


def member(place):
    return place % 4 * 8 + 7 - place // 4


ORDER = [member(p) for p in range(SPANS)]
PLACE = [ORDER.index(q) for q in range(SPANS)]
FAR = 128 // FINE

ON_CHIP = pl.BlockSpec(memory_space=pltpu.VMEM)
HBM = pl.BlockSpec(memory_space=pltpu.HBM)


def pack_kernel(noise_hbm, inc_hbm, factor_hbm, scale_hbm, out, strip_ref, small_ref, scale_ref, x_ref, inc_ref, factor_ref, lines, scr, sems):
    get_noise = pltpu.make_async_copy(noise_hbm, x_ref, sems.at[0])
    get_inc = pltpu.make_async_copy(inc_hbm, inc_ref, sems.at[1])
    get_factor = pltpu.make_async_copy(factor_hbm, factor_ref, sems.at[2])
    get_scale = pltpu.make_async_copy(scale_hbm, scale_ref, sems.at[3])
    get_factor.start()
    get_inc.start()
    get_noise.start()
    get_scale.start()

    get_factor.wait()
    lines[...] = factor_ref[...].astype(jnp.float32)
    row = lax.broadcasted_iota(jnp.int32, (16, 128), 0)
    col = lax.broadcasted_iota(jnp.int32, (16, 128), 1)
    keep = col >= row
    before = jnp.zeros((16, 128), jnp.float32)
    for tile in range(TILES):
        line = jnp.broadcast_to(lines[tile:tile + 1, :], (16, 128))
        now = pltpu.roll(line, 0, 1, stride=1, stride_axis=0)
        strip_ref[tile] = jnp.where(keep, now, before).astype(jnp.bfloat16)
        before = now

    get_inc.wait()
    inc = inc_ref[...].astype(jnp.float32).astype(jnp.bfloat16)
    small_ref[...] = inc
    inc = jnp.concatenate([inc, jnp.zeros((32, STEPS), jnp.bfloat16)], axis=0)
    ones = jnp.ones((8, STEPS), jnp.bfloat16)
    sums = lax.dot_general(ones, inc, (((1,), (1,)), ((), ())), preferred_element_type=jnp.float32)
    high = jnp.floor(sums * (1.0 / 64.0))
    low = sums - 64.0 * high
    zero = jnp.zeros((8, 128), jnp.float32)
    get_noise.wait()
    get_scale.wait()
    for g in range(4):
        base = 8 * g * ROWS
        for h in range(2):
            for c in range(3):
                top = 32 * c + 8 * g
                for k in range(4):
                    col = 256 * k + 128 * h
                    tile = x_ref[top:top + 8, col:col + 128].astype(jnp.float32)
                    scr[h, pl.ds(base + 3 * k + c, 8, stride=ROWS), :] = tile
            for r, v in ((12, high), (13, low), (14, zero), (15, zero)):
                scr[h, pl.ds(base + r, 8, stride=ROWS), :] = v if h == 0 else zero
            tile = scr[h, base:base + 8 * ROWS, :].astype(jnp.bfloat16)
            out[8 * g:8 * g + 8, :, 128 * h:128 * h + 128] = tile.reshape(8, ROWS, 128)


def running(inc):
    row = lax.broadcasted_iota(jnp.int32, (BLK, BLK), 0)
    col = lax.broadcasted_iota(jnp.int32, (BLK, BLK), 1)
    tri = jnp.where(row <= col, 1.0, 0.0).astype(jnp.bfloat16)
    full = jnp.ones((BLK, BLK), jnp.bfloat16)
    for k in range(4):
        mat = jnp.concatenate([full] * k + [tri], axis=0)
        yield k, jnp.dot(inc[:, :BLK * (k + 1)], mat, preferred_element_type=jnp.float32)


def conv_kernel(recv_ref, strip, out_ref, xf, xs, acc):
    xf[:, 0:SHIFT, :] = jnp.zeros((2, SHIFT, 128), jnp.float32)
    for h in range(2):
        lanes = slice(128 * h, 128 * h + 128)
        for q in range(SPANS):
            xf[h, SHIFT + 12 * q:SHIFT + 12 * q + 12, :] = recv_ref[PLACE[q], 0:12, lanes].astype(jnp.float32)
    for e in range(FINE):
        for h in range(2):
            lane = BLK * e + 128 * h
            xs[:, lane:lane + 128] = xf[h, SHIFT - 3 * e:SHIFT - 3 * e + 384, :].astype(jnp.bfloat16)

    col = lax.broadcasted_iota(jnp.int32, (16, 128), 1)
    zero = jnp.zeros((16, 128), jnp.bfloat16)

    def rolls(tile):
        if tile < 0:
            return [zero] * 8
        base = strip[tile]
        return [base] + [pltpu.roll(base, 16 * i, 1) for i in range(1, 8)]

    def square(now, before):
        return jnp.concatenate(
            [now[0]] + [jnp.where(col >= 16 * i, now[i], before[i]) for i in range(1, 8)], axis=0)

    for far in range(FAR):
        rows = 384 - SHIFT * far
        first = 2 * FINE * far
        rolled = {tile: rolls(tile) for tile in range(first - 2, first + 2 * FINE)}
        squares = {tile: square(rolled[tile], rolled[tile - 1]) for tile in range(first - 1, first + 2 * FINE)}
        parts = []
        for e in range(FINE):
            at = first + 2 * e
            parts.append(jnp.concatenate([squares[at], squares[at + 1]], axis=1))
            parts.append(jnp.concatenate([squares[at - 1], squares[at]], axis=1))
        weights = jnp.concatenate(parts, axis=0)
        part = jnp.dot(xs[0:rows, :], weights, preferred_element_type=jnp.float32)
        if far == 0:
            acc[...] = part
        else:
            acc[SHIFT * far:, :] += part
        for q in range(4 * far, 4 * far + 4):
            top, low = slice(12 * q, 12 * q + 8), slice(12 * q + 8, 12 * q + 12)
            values = [acc[top, 0:128], acc[top, 128:256], jnp.concatenate([acc[low, 0:128], acc[low, 128:256]], axis=0)]
            most = jnp.maximum(jnp.maximum(jnp.abs(values[0]), jnp.abs(values[1])), jnp.abs(values[2]))
            most = jnp.maximum(jnp.max(most, axis=1, keepdims=True), TINY)
            power = jnp.broadcast_to(jnp.ceil(jnp.log2(most) - LOG_TOP), (8, 128))
            unit = jnp.exp2(-power)
            coded = [jnp.round(v * unit) for v in values] + [power]
            for half in range(2):
                rows16 = jnp.concatenate(coded[2 * half:2 * half + 2], axis=0)
                out_ref[PLACE[q], 16 * half:16 * half + 16, :] = rows16.astype(jnp.int32).astype(jnp.int16)


def carry_kernel(recv_ref, small_ref, scale_ref, carry_ref, group_ref, wide_ref):
    sums = recv_ref[:, 12:14, 0:128].astype(jnp.float32)
    high = sums[:, 0, :].astype(jnp.bfloat16)
    low = sums[:, 1, :].astype(jnp.bfloat16)
    place = lax.broadcasted_iota(jnp.int32, (SPANS, 128), 0)
    mask = jnp.where(member(place) < lax.axis_index("tm"), 1.0, 0.0).astype(jnp.bfloat16)
    dims = (((0,), (0,)), ((), ()))
    carried = 64.0 * lax.dot_general(high, mask, dims, preferred_element_type=jnp.float32)
    carried = (carried + lax.dot_general(low, mask, dims, preferred_element_type=jnp.float32))[:CELLS]
    carry_ref[...] = carried.astype(jnp.int32)
    before = jnp.sum(carried, axis=0, keepdims=True)
    for k, part in running(small_ref[...]):
        total = jnp.sum(part, axis=0, keepdims=True)
        for h in range(2):
            group_ref[2 * k + h:2 * k + h + 1, :] = (total[:, 128 * h:128 * h + 128] + before).astype(jnp.int32)
    wide_ref[...] = jnp.transpose(jnp.broadcast_to(scale_ref[...], (128, CELLS)))


def counts_kernel(small_ref, carry_ref, out_ref):
    carry = carry_ref[...]
    for k, part in running(small_ref[...]):
        for h in range(2):
            lane = BLK * k + 128 * h
            out_ref[:, lane:lane + 128] = part[:, 128 * h:128 * h + 128].astype(jnp.int32) + carry


def spread_kernel(back_ref, scale_ref, group_ref, other_ref, out_hbm, total_hbm, flat, out, total, sems):
    total[...] = group_ref[...] + other_ref[...]
    copies = [pltpu.make_async_copy(total, total_hbm, sems.at[0])]
    copies[0].start()
    for g in range(4):
        base = 256 * g
        flat[base:base + 256, :] = back_ref[base:base + 256, :].astype(jnp.int32).astype(jnp.float32)
        units = [jnp.exp2(flat[pl.ds(base + 24 + j, 8, stride=32), :]) for j in range(8)]
        for c in range(3):
            top = 32 * c + 8 * g
            scale = scale_ref[top:top + 8, :]
            for k in range(4):
                r = 3 * k + c
                for h in range(2):
                    sub = 8 * h + r if r < 8 else 8 + 4 * h + r
                    tile = flat[pl.ds(base + sub, 8, stride=32), :] * units[sub % 8]
                    out[top:top + 8, 256 * k + 128 * h:256 * k + 128 * h + 128] = tile * scale
            rows = pl.ds(top, 8)
            copies.append(pltpu.make_async_copy(out.at[rows], out_hbm.at[rows], sems.at[len(copies)]))
            copies[-1].start()
    for copy in copies:
        copy.wait()


def call(kernel, outs, args, in_specs=None, out_specs=None, scratch=(), **rest):
    return pl.pallas_call(
        kernel,
        out_shape=outs,
        in_specs=in_specs or [ON_CHIP] * len(args),
        out_specs=out_specs or jax.tree.map(lambda _: ON_CHIP, outs),
        scratch_shapes=scratch,
        compiler_params=pltpu.CompilerParams(vmem_limit_bytes=24 << 20),
        **rest,
    )(*args)


def on_chip(x):
    return pltpu.with_memory_space_constraint(x, pltpu.VMEM)


def in_hbm(x):
    return pltpu.with_memory_space_constraint(x, pltpu.HBM)


def steps(increments, noise, noise_scale, factor):
    f32, i32, bf16 = jnp.float32, jnp.int32, jnp.bfloat16
    sds = jax.ShapeDtypeStruct
    dma = pltpu.SemaphoreType.DMA
    chip = pltpu.VMEM
    message, strips, small, scales = call(
        pack_kernel, (sds((SPANS, ROWS, BLK), bf16), chip((TILES, 16, 128), bf16), chip((CELLS, STEPS), bf16), chip((1, CELLS), f32)),
        (in_hbm(noise), in_hbm(increments), in_hbm(factor.reshape(TILES, 128)), in_hbm(noise_scale.reshape(1, CELLS))),
        in_specs=[HBM] * 4,
        scratch=[pltpu.VMEM((CELLS, STEPS), bf16), pltpu.VMEM((CELLS, STEPS), i32), pltpu.VMEM((TILES, 128), bf16),
                 pltpu.VMEM((TILES, 128), f32), pltpu.VMEM((2, SPANS * ROWS, 128), f32), dma((4,))],
    )
    received = lax.all_to_all(message, "tm", 0, 0, tiled=True, axis_index_groups=[ORDER])
    sent = call(
        conv_kernel, sds((SPANS, 32, 128), jnp.int16), (on_chip(received), on_chip(strips)),
        scratch=[
            pltpu.VMEM((2, SHIFT + 384, 128), f32),
            pltpu.VMEM((384, FINE * BLK), bf16),
            pltpu.VMEM((384, BLK), f32),
        ],
    )
    back = lax.all_to_all(sent, "tm", 0, 0, tiled=True, axis_index_groups=[ORDER])
    carry, group, wide = call(
        carry_kernel, (sds((CELLS, 128), i32), sds((8, 128), i32), chip((CELLS, 128), f32)),
        (received, small, on_chip(scales)))
    group = group + lax.ppermute(group, "cell", [(i, i ^ 1) for i in range(8)])
    group = group + lax.ppermute(group, "cell", [(i, i ^ 2) for i in range(8)])
    other = lax.ppermute(group, "cell", [(i, i ^ 6) for i in range(8)])
    counts = call(counts_kernel, sds((CELLS, STEPS), i32), (small, carry))
    correlated, total = call(
        spread_kernel, (sds((CELLS, STEPS), f32), sds((8, 128), i32)),
        (on_chip(back.reshape(SPANS * 32, 128)), on_chip(wide), on_chip(group), on_chip(other)),
        out_specs=(HBM, HBM),
        scratch=[pltpu.VMEM((SPANS * 32, 128), f32), pltpu.VMEM((CELLS, STEPS), f32), pltpu.VMEM((8, 128), i32), dma((13,))],
    )
    return counts, correlated, total.reshape(STEPS)


def solution(mesh):
    return jax.shard_map(
        steps,
        mesh=mesh,
        in_specs=(P("cell", "tm"), P("cell", "tm"), P("cell"), P()),
        out_specs=(P("cell", "tm"), P("cell", "tm"), P("tm")),
        check_vma=False,
    )
```

```python
import math

import jax
import jax.numpy as jnp
from jax import lax
from jax.experimental import pallas as pl
from jax.experimental.pallas import tpu as pltpu
from jax.sharding import PartitionSpec as P

SPANS = 32
CELLS = 96
STEPS = 1024
BLK = 256
ROWS = 16
TILES = 256
FINE = 8
SHIFT = 3 * FINE
LOG_TOP = math.log2(32000.0)
TINY = 2.0 ** -100


def member(place):
    return place % 4 * 8 + (place // 4 + 7) % 8


ORDER = [member(p) for p in range(SPANS)]
PLACE = [ORDER.index(q) for q in range(SPANS)]
FAR = 128 // FINE

ON_CHIP = pl.BlockSpec(memory_space=pltpu.VMEM)
HBM = pl.BlockSpec(memory_space=pltpu.HBM)


def pack_kernel(noise_hbm, inc_hbm, factor_hbm, scale_hbm, out, strip_ref, small_ref, scale_ref, x_ref, inc_ref, factor_ref, lines, scr, sems):
    get_noise = pltpu.make_async_copy(noise_hbm, x_ref, sems.at[0])
    get_inc = pltpu.make_async_copy(inc_hbm, inc_ref, sems.at[1])
    get_factor = pltpu.make_async_copy(factor_hbm, factor_ref, sems.at[2])
    get_scale = pltpu.make_async_copy(scale_hbm, scale_ref, sems.at[3])
    get_factor.start()
    get_inc.start()
    get_noise.start()
    get_scale.start()

    get_factor.wait()
    lines[...] = factor_ref[...].astype(jnp.float32)
    row = lax.broadcasted_iota(jnp.int32, (16, 128), 0)
    col = lax.broadcasted_iota(jnp.int32, (16, 128), 1)
    keep = col >= row
    before = jnp.zeros((16, 128), jnp.float32)
    for tile in range(TILES):
        line = jnp.broadcast_to(lines[tile:tile + 1, :], (16, 128))
        now = pltpu.roll(line, 0, 1, stride=1, stride_axis=0)
        strip_ref[tile] = jnp.where(keep, now, before).astype(jnp.bfloat16)
        before = now

    get_inc.wait()
    inc = inc_ref[...].astype(jnp.float32).astype(jnp.bfloat16)
    small_ref[...] = inc
    inc = jnp.concatenate([inc, jnp.zeros((32, STEPS), jnp.bfloat16)], axis=0)
    ones = jnp.ones((8, STEPS), jnp.bfloat16)
    sums = lax.dot_general(ones, inc, (((1,), (1,)), ((), ())), preferred_element_type=jnp.float32)
    high = jnp.floor(sums * (1.0 / 64.0))
    low = sums - 64.0 * high
    zero = jnp.zeros((8, 128), jnp.float32)
    get_noise.wait()
    get_scale.wait()
    for g in range(4):
        base = 8 * g * ROWS
        for h in range(2):
            for c in range(3):
                top = 32 * c + 8 * g
                for k in range(4):
                    col = 256 * k + 128 * h
                    tile = x_ref[top:top + 8, col:col + 128].astype(jnp.float32)
                    scr[h, pl.ds(base + 3 * k + c, 8, stride=ROWS), :] = tile
            for r, v in ((12, high), (13, low), (14, zero), (15, zero)):
                scr[h, pl.ds(base + r, 8, stride=ROWS), :] = v if h == 0 else zero
            tile = scr[h, base:base + 8 * ROWS, :].astype(jnp.bfloat16)
            out[8 * g:8 * g + 8, :, 128 * h:128 * h + 128] = tile.reshape(8, ROWS, 128)


def running(inc):
    row = lax.broadcasted_iota(jnp.int32, (BLK, BLK), 0)
    col = lax.broadcasted_iota(jnp.int32, (BLK, BLK), 1)
    tri = jnp.where(row <= col, 1.0, 0.0).astype(jnp.bfloat16)
    full = jnp.ones((BLK, BLK), jnp.bfloat16)
    for k in range(4):
        mat = jnp.concatenate([full] * k + [tri], axis=0)
        yield k, jnp.dot(inc[:, :BLK * (k + 1)], mat, preferred_element_type=jnp.float32)


def conv_kernel(recv_ref, strip, out_ref, xf, xs, acc):
    xf[:, 0:SHIFT, :] = jnp.zeros((2, SHIFT, 128), jnp.float32)
    for h in range(2):
        lanes = slice(128 * h, 128 * h + 128)
        for q in range(SPANS):
            xf[h, SHIFT + 12 * q:SHIFT + 12 * q + 12, :] = recv_ref[PLACE[q], 0:12, lanes].astype(jnp.float32)
    for e in range(FINE):
        for h in range(2):
            lane = BLK * e + 128 * h
            xs[:, lane:lane + 128] = xf[h, SHIFT - 3 * e:SHIFT - 3 * e + 384, :].astype(jnp.bfloat16)

    col = lax.broadcasted_iota(jnp.int32, (16, 128), 1)
    zero = jnp.zeros((16, 128), jnp.bfloat16)

    def rolls(tile):
        if tile < 0:
            return [zero] * 8
        base = strip[tile]
        return [base] + [pltpu.roll(base, 16 * i, 1) for i in range(1, 8)]

    def square(now, before):
        return jnp.concatenate(
            [now[0]] + [jnp.where(col >= 16 * i, now[i], before[i]) for i in range(1, 8)], axis=0)

    for far in range(FAR):
        rows = 384 - SHIFT * far
        first = 2 * FINE * far
        rolled = {tile: rolls(tile) for tile in range(first - 2, first + 2 * FINE)}
        squares = {tile: square(rolled[tile], rolled[tile - 1]) for tile in range(first - 1, first + 2 * FINE)}
        parts = []
        for e in range(FINE):
            at = first + 2 * e
            parts.append(jnp.concatenate([squares[at], squares[at + 1]], axis=1))
            parts.append(jnp.concatenate([squares[at - 1], squares[at]], axis=1))
        weights = jnp.concatenate(parts, axis=0)
        part = jnp.dot(xs[0:rows, :], weights, preferred_element_type=jnp.float32)
        if far == 0:
            acc[...] = part
        else:
            acc[SHIFT * far:, :] += part
        for q in range(SPANS // FAR * far, SPANS // FAR * (far + 1)):
            top, low = slice(12 * q, 12 * q + 8), slice(12 * q + 8, 12 * q + 12)
            values = [acc[top, 0:128], acc[top, 128:256], jnp.concatenate([acc[low, 0:128], acc[low, 128:256]], axis=0)]
            most = jnp.maximum(jnp.maximum(jnp.abs(values[0]), jnp.abs(values[1])), jnp.abs(values[2]))
            most = jnp.maximum(jnp.max(most, axis=1, keepdims=True), TINY)
            power = jnp.broadcast_to(jnp.ceil(jnp.log2(most) - LOG_TOP), (8, 128))
            unit = jnp.exp2(-power)
            coded = [jnp.round(v * unit) for v in values] + [power]
            for half in range(2):
                rows16 = jnp.concatenate(coded[2 * half:2 * half + 2], axis=0)
                out_ref[PLACE[q], 16 * half:16 * half + 16, :] = rows16.astype(jnp.int32).astype(jnp.int16)


def carry_kernel(recv_ref, small_ref, scale_ref, carry_ref, group_ref, wide_ref):
    sums = recv_ref[:, 12:14, 0:128].astype(jnp.float32)
    high = sums[:, 0, :].astype(jnp.bfloat16)
    low = sums[:, 1, :].astype(jnp.bfloat16)
    place = lax.broadcasted_iota(jnp.int32, (SPANS, 128), 0)
    mask = jnp.where(member(place) < lax.axis_index("tm"), 1.0, 0.0).astype(jnp.bfloat16)
    dims = (((0,), (0,)), ((), ()))
    carried = 64.0 * lax.dot_general(high, mask, dims, preferred_element_type=jnp.float32)
    carried = (carried + lax.dot_general(low, mask, dims, preferred_element_type=jnp.float32))[:CELLS]
    carry_ref[...] = carried.astype(jnp.int32)
    before = jnp.sum(carried, axis=0, keepdims=True)
    for k, part in running(small_ref[...]):
        total = jnp.sum(part, axis=0, keepdims=True)
        for h in range(2):
            group_ref[2 * k + h:2 * k + h + 1, :] = (total[:, 128 * h:128 * h + 128] + before).astype(jnp.int32)
    wide_ref[...] = jnp.transpose(jnp.broadcast_to(scale_ref[...], (128, CELLS)))


def counts_kernel(small_ref, carry_ref, out_ref):
    carry = carry_ref[...]
    for k, part in running(small_ref[...]):
        for h in range(2):
            lane = BLK * k + 128 * h
            out_ref[:, lane:lane + 128] = part[:, 128 * h:128 * h + 128].astype(jnp.int32) + carry


def spread_kernel(back_ref, scale_ref, group_ref, other_ref, out_hbm, total_hbm, flat, out, total, sems):
    total[...] = group_ref[...] + other_ref[...]
    copies = [pltpu.make_async_copy(total, total_hbm, sems.at[0])]
    copies[0].start()
    for g in range(4):
        base = 256 * g
        flat[base:base + 256, :] = back_ref[base:base + 256, :].astype(jnp.int32).astype(jnp.float32)
        units = [jnp.exp2(flat[pl.ds(base + 24 + j, 8, stride=32), :]) for j in range(8)]
        for c in range(3):
            top = 32 * c + 8 * g
            scale = scale_ref[top:top + 8, :]
            for k in range(4):
                r = 3 * k + c
                for h in range(2):
                    sub = 8 * h + r if r < 8 else 8 + 4 * h + r
                    tile = flat[pl.ds(base + sub, 8, stride=32), :] * units[sub % 8]
                    out[top:top + 8, 256 * k + 128 * h:256 * k + 128 * h + 128] = tile * scale
            rows = pl.ds(top, 8)
            copies.append(pltpu.make_async_copy(out.at[rows], out_hbm.at[rows], sems.at[len(copies)]))
            copies[-1].start()
    for copy in copies:
        copy.wait()


def call(kernel, outs, args, in_specs=None, out_specs=None, scratch=(), **rest):
    return pl.pallas_call(
        kernel,
        out_shape=outs,
        in_specs=in_specs or [ON_CHIP] * len(args),
        out_specs=out_specs or jax.tree.map(lambda _: ON_CHIP, outs),
        scratch_shapes=scratch,
        compiler_params=pltpu.CompilerParams(vmem_limit_bytes=24 << 20),
        **rest,
    )(*args)


def on_chip(x):
    return pltpu.with_memory_space_constraint(x, pltpu.VMEM)


def in_hbm(x):
    return pltpu.with_memory_space_constraint(x, pltpu.HBM)


def steps(increments, noise, noise_scale, factor):
    f32, i32, bf16 = jnp.float32, jnp.int32, jnp.bfloat16
    sds = jax.ShapeDtypeStruct
    dma = pltpu.SemaphoreType.DMA
    chip = pltpu.VMEM
    message, strips, small, scales = call(
        pack_kernel, (sds((SPANS, ROWS, BLK), bf16), chip((TILES, 16, 128), bf16), chip((CELLS, STEPS), bf16), chip((1, CELLS), f32)),
        (in_hbm(noise), in_hbm(increments), in_hbm(factor.reshape(TILES, 128)), in_hbm(noise_scale.reshape(1, CELLS))),
        in_specs=[HBM] * 4,
        scratch=[pltpu.VMEM((CELLS, STEPS), bf16), pltpu.VMEM((CELLS, STEPS), i32), pltpu.VMEM((TILES, 128), bf16),
                 pltpu.VMEM((TILES, 128), f32), pltpu.VMEM((2, SPANS * ROWS, 128), f32), dma((4,))],
    )
    received = lax.all_to_all(message, "tm", 0, 0, tiled=True, axis_index_groups=[ORDER])
    sent = call(
        conv_kernel, sds((SPANS, 32, 128), jnp.int16), (on_chip(received), on_chip(strips)),
        scratch=[
            pltpu.VMEM((2, SHIFT + 384, 128), f32),
            pltpu.VMEM((384, FINE * BLK), bf16),
            pltpu.VMEM((384, BLK), f32),
        ],
    )
    back = lax.all_to_all(sent, "tm", 0, 0, tiled=True, axis_index_groups=[ORDER])
    carry, group, wide = call(
        carry_kernel, (sds((CELLS, 128), i32), sds((8, 128), i32), chip((CELLS, 128), f32)),
        (received, small, on_chip(scales)))
    group = group + lax.ppermute(group, "cell", [(i, i ^ 1) for i in range(8)])
    group = group + lax.ppermute(group, "cell", [(i, i ^ 2) for i in range(8)])
    other = lax.ppermute(group, "cell", [(i, i ^ 6) for i in range(8)])
    counts = call(counts_kernel, sds((CELLS, STEPS), i32), (small, carry))
    correlated, total = call(
        spread_kernel, (sds((CELLS, STEPS), f32), sds((8, 128), i32)),
        (on_chip(back.reshape(SPANS * 32, 128)), on_chip(wide), on_chip(group), on_chip(other)),
        out_specs=(HBM, HBM),
        scratch=[pltpu.VMEM((SPANS * 32, 128), f32), pltpu.VMEM((CELLS, STEPS), f32), pltpu.VMEM((8, 128), i32), dma((13,))],
    )
    return counts, correlated, total.reshape(STEPS)


def solution(mesh):
    return jax.shard_map(
        steps,
        mesh=mesh,
        in_specs=(P("cell", "tm"), P("cell", "tm"), P("cell"), P()),
        out_specs=(P("cell", "tm"), P("cell", "tm"), P("tm")),
        check_vma=False,
    )
```
